512 devices in a mesh: wide: 64 (over x, z_lo, core), narrow: 8 (over z_hi, y).
Axes of the slice: x: 4, y: 4, z: 16 (z_hi: 2, z_lo: 8; z = z_hi * 8 + z_lo), core: 2. Of those that a mesh axis runs over, the one named last changes fastest.
Arguments:
- vectors: float32 [4096, 65536], P('narrow', 'wide'), may hold values from -6 to 6
- weights: bfloat16 [5, 256, 256, 512], P(None, 'wide', 'narrow'), may hold values from -0.25 to 0.25
Outputs:
- transformed: float32 [4096, 65536], P('narrow', 'wide')
The draws below stay inside these ranges and needn't reach their ends.
All inputs are finite; a program needn't handle non-finite values.
Results may differ from the reference program's by a relative error of at most 0.0003.
Values may be sent and summed in bfloat16 or wider, within the bound.
No kernel may reach another device: no remote copies, remote signals or barrier semaphores. Data moves between devices by JAX's collectives and lax.ppermute only.
A program may use at most 64 MiB of HBM per device.

```python
import jax
import jax.numpy as jnp
from jax import lax

BLK_DEV = 4
BLOCK = 256
LEVELS = 5
VECTORS = 4096
BLOCKS = 256
COEFFS = 65536
N_WIDE = 64


def steps_of(key, shape, shards, low, top_value):
    gain, own = 1.0, jax.random.fold_in(key, 6)
    for position, shards_of in shards:
        steps = jnp.exp(jax.random.uniform(jax.random.fold_in(own, position), (shards_of,), jnp.float32, low / len(shards), top_value / len(shards)))
        gain = gain * jnp.repeat(steps, shape[position] // shards_of).reshape([-1 if axis == position else 1 for axis in range(len(shape))])
    return gain


def noise(stream_key, dims, spread, limit, shards=(), dtype=jnp.bfloat16):
    level = steps_of(stream_key, dims, shards, -0.22, 0.18) if shards else 1.0
    array = jax.random.normal(stream_key, dims, jnp.float32) * spread * level
    return jnp.minimum(jnp.maximum(array, -limit), limit).astype(dtype)


def setup_inputs(seed: int = 0) -> dict:
    arg_keys = jax.random.split(jax.random.key(seed), 3)
    vectors = noise(arg_keys[0], (VECTORS, COEFFS), 1.0, 6.0, ((0, 8), (1, 64)), jnp.float32)
    weights = noise(arg_keys[1], (LEVELS, BLOCKS, BLOCK, 2 * BLOCK), (2 * BLOCK) ** -0.5, 0.25, ((1, 64), (2, 8)))
    return dict(vectors=vectors, weights=weights)


def apply_level(current, matrices, level_bit):
    columns, block_count, block_size = current.shape
    stride = 1 << level_bit
    grouped = current.reshape(columns, block_count // (2 * stride), 2, stride, block_size)
    paired = jnp.concatenate([grouped[:, :, 0], grouped[:, :, 1]], -1)
    matrix = matrices.astype(jnp.float32).reshape(block_count // (2 * stride), 2, stride, block_size, 2 * block_size)
    result = jnp.einsum('vaji,asjoi->vasjo', paired, matrix, precision=lax.Precision.HIGHEST)
    return result.reshape(columns, block_count, block_size)


def reference(vectors, weights):
    local_bits = BLK_DEV.bit_length() - 1
    wide_top = N_WIDE.bit_length() - 1
    level_bits = [0, 1, local_bits, local_bits + wide_top // 2, local_bits + wide_top - 1]
    block_size = weights.shape[2]
    current = vectors.reshape(vectors.shape[0], vectors.shape[1] // block_size, block_size)
    for level_index in range(LEVELS):
        current = apply_level(current, weights[level_index], level_bits[level_index])
    return current.reshape(vectors.shape)
```

```python
import functools

import jax
import jax.numpy as jnp
from jax import lax
from jax.experimental import pallas as pl
from jax.experimental.pallas import tpu as pltpu
from jax.sharding import Mesh
from jax.sharding import PartitionSpec as P

NARROW = ("narrow_0", "narrow_1")
FLOOR = 2.0 ** -3.875
SPAN = 2.0 ** 3.875 - 2.0 ** -3.875
LANES = 128
SCALE_ROWS = 16


def swapped(shard, axis, apart):
    return lax.ppermute(shard, axis, [(i, i ^ 1 << apart) for i in range(lax.axis_size(axis))])


def assemble(matrix, own_ref, other_ref, half):
    parts, _, blocks, rows, _ = own_ref.shape
    for part in range(parts):
        for block in range(blocks):
            for ref, side in ((own_ref, half), (other_ref, 1 - half)):
                start = pl.multiple_of(side * (parts * rows) + part * rows, rows)
                matrix[block, pl.ds(start, rows), :] = ref[part, 0, block]


def split(x):
    high = x.astype(jnp.bfloat16)
    return high, (x - high.astype(jnp.float32)).astype(jnp.bfloat16)


def product(parts, matrix):
    dims = (((1,), (1,)), ((), ()))
    dots = [lax.dot_general(part, matrix, dims, preferred_element_type=jnp.float32) for part in parts]
    return dots[0] + dots[1]


def encode(value, out_ref):
    rows, columns = value.shape
    top = jnp.max(jnp.abs(value), axis=1, keepdims=True)
    top = jnp.maximum(jnp.broadcast_to(top, (rows, LANES)) * 1.01, 1e-30).astype(jnp.bfloat16)
    top = top.astype(jnp.float32)
    out_ref[pl.ds(rows * (columns // LANES), SCALE_ROWS), :] = top.T[:SCALE_ROWS].astype(jnp.bfloat16)
    gain = SPAN / top
    for tile in range(columns // LANES):
        x = value[:, tile * LANES:(tile + 1) * LANES]
        t = jnp.abs(x) * gain + FLOOR
        for _ in range(5):
            t = t * t
        out_ref[pl.ds(tile * rows, rows), :] = jnp.where(x < 0, -t, t).astype(jnp.bfloat16)


def decode(code_ref, rows, columns):
    tiles = columns // LANES
    top = code_ref[pl.ds(rows * tiles, SCALE_ROWS), :].astype(jnp.float32)
    gain = jnp.broadcast_to(top[:1], (LANES, LANES)).T[:rows] * (1.0 / SPAN)
    values = []
    for tile in range(tiles):
        g = code_ref[pl.ds(tile * rows, rows), :].astype(jnp.float32)
        t = jnp.exp(jnp.log(jnp.abs(g)) * (1.0 / 32.0))
        y = (t - FLOOR) * gain
        values.append(jnp.where(g < 0, -y, y))
    return jnp.concatenate(values, axis=1)


def blocks_of(value, count, size):
    return [split(value[:, k * size:(k + 1) * size]) for k in range(count)]


def local_body(bits_ref, x_ref, own0, other0, own1, other1, out_ref, matrix0, matrix1):
    @pl.when(pl.program_id(0) == 0)
    def _():
        assemble(matrix0, own0, other0, bits_ref[0])
        assemble(matrix1, own1, other1, bits_ref[0])

    count, size = matrix0.shape[:2]
    value = x_ref[...]
    for level, matrix in enumerate((matrix0, matrix1)):
        parts = blocks_of(value, count, size)
        outs = []
        for k in range(count):
            low, high = parts[k & ~(1 << level)], parts[k | 1 << level]
            outs.append(product(low, matrix[k, :, :size]) + product(high, matrix[k, :, size:]))
        value = jnp.concatenate(outs, axis=1)
    out_ref[...] = value


def cross_level(mine, partner, matrix, upper, count, size):
    own_parts, partner_parts = blocks_of(mine, count, size), blocks_of(partner, count, size)
    own_at = pl.multiple_of(upper * size, size)
    partner_at = pl.multiple_of((1 - upper) * size, size)
    outs = []
    for k in range(count):
        outs.append(
            product(own_parts[k], matrix[k, :, pl.ds(own_at, size)])
            + product(partner_parts[k], matrix[k, :, pl.ds(partner_at, size)])
        )
    return jnp.concatenate(outs, axis=1)


def core_body(bits_ref, mine_ref, partner_ref, own, other, out_ref, code_ref, matrix):
    assemble(matrix, own, other, bits_ref[0])
    count, size = matrix.shape[:2]
    value = cross_level(mine_ref[...], partner_ref[...], matrix, bits_ref[1], count, size)
    out_ref[...] = value
    encode(value, code_ref)


def middle_body(bits_ref, mine_ref, partner_ref, own, other, out_ref, code_ref, matrix):
    assemble(matrix, own, other, bits_ref[0])
    count, size = matrix.shape[:2]
    partner = decode(partner_ref, *mine_ref.shape)
    value = cross_level(mine_ref[...], partner, matrix, bits_ref[2], count, size)
    out_ref[...] = value
    encode(value, code_ref)


def last_body(bits_ref, mine_ref, partner_ref, own, other, *rest):
    out_ref, matrix = rest[-2:]
    assemble(matrix, own, other, bits_ref[0])
    count, size = matrix.shape[:2]
    partner = decode(partner_ref, *mine_ref.shape)
    out_ref[...] = cross_level(mine_ref[...], partner, matrix, bits_ref[3], count, size)


def on_device(vectors, weights, chunks=4):
    columns, coeffs = vectors.shape
    _, count, share, width = weights.shape
    size = width // 2
    parts = lax.axis_size("narrow_1")
    rows = columns // chunks
    code_rows = rows * (coeffs // LANES) + SCALE_ROWS
    wide_top = lax.axis_size("wide").bit_length() - 1
    wide_bits = [0, wide_top // 2, wide_top - 1]
    place = lax.axis_index("wide")
    bits = jnp.stack([lax.axis_index("narrow_0")] + [place >> bit & 1 for bit in wide_bits])

    first, second = weights[:3], weights[3:]
    own_first = lax.all_gather(first, "narrow_1")
    other_shard = swapped(first, "narrow_0", 0)
    other_first = lax.all_gather(other_shard, "narrow_1")
    second_later, _ = lax.optimization_barrier((second, other_shard))
    own_second = lax.all_gather(second, "narrow_1")
    other_second = lax.all_gather(swapped(second_later, "narrow_0", 0), "narrow_1")

    def matrix_spec(level):
        return pl.BlockSpec((parts, 1, count, share, width), lambda i, bits: (0, level, 0, 0, 0))

    matrix_scratch = pltpu.VMEM((count, size, width), jnp.bfloat16)

    def cost(rows_done, levels, bytes_accessed):
        return pl.CostEstimate(
            flops=4 * levels * rows_done * coeffs * width, bytes_accessed=bytes_accessed, transcendentals=0
        )

    matrix_bytes = 2 * count * size * width

    def call(body, grid, in_specs, out_specs, out_shape, scratch, estimate, aliases={}):
        return pl.pallas_call(
            body,
            grid_spec=pltpu.PrefetchScalarGridSpec(
                num_scalar_prefetch=1, grid=grid, in_specs=in_specs, out_specs=out_specs, scratch_shapes=scratch
            ),
            out_shape=out_shape,
            input_output_aliases=aliases,
            cost_estimate=estimate,
            compiler_params=pltpu.CompilerParams(vmem_limit_bytes=48 << 20),
        )

    def row_spec(index):
        return pl.BlockSpec((rows, coeffs), lambda i, bits: (index, 0))

    moving = pl.BlockSpec((rows, coeffs), lambda i, bits: (i, 0))
    whole = pl.BlockSpec((rows, coeffs), lambda i, bits: (0, 0))
    code_spec = pl.BlockSpec((code_rows, LANES), lambda i, bits: (0, 0))
    code_shape = jax.ShapeDtypeStruct((code_rows, LANES), jnp.bfloat16)
    chunk_shape = jax.ShapeDtypeStruct((rows, coeffs), jnp.float32)

    current = call(
        local_body, (chunks,), [moving] + [matrix_spec(level) for level in (0, 0, 1, 1)], moving,
        jax.ShapeDtypeStruct((columns, coeffs), jnp.float32), [matrix_scratch] * 2,
        cost(columns, 2, 8 * columns * coeffs + 2 * matrix_bytes),
    )(bits, vectors, own_first, other_first, own_first, other_first)
    partner = swapped(current, "wide", wide_bits[0])

    pieces = []
    for c in range(chunks):
        mine, code = call(
            core_body, (1,), [row_spec(c), row_spec(c), matrix_spec(2), matrix_spec(2)], [whole, code_spec],
            [chunk_shape, code_shape], [matrix_scratch], cost(rows, 1, 14 * rows * coeffs + matrix_bytes),
        )(bits, current, partner, own_first, other_first)
        pieces.append((mine, swapped(code, "wide", wide_bits[1])))
    later = []
    for mine, code in pieces:
        mine, code = call(
            middle_body, (1,), [whole, code_spec, matrix_spec(0), matrix_spec(0)], [whole, code_spec],
            [chunk_shape, code_shape], [matrix_scratch], cost(rows, 1, 12 * rows * coeffs + matrix_bytes),
        )(bits, mine, code, own_second, other_second)
        later.append((mine, swapped(code, "wide", wide_bits[2])))
    out = None
    for c, (mine, code) in enumerate(later):
        operands = [bits, mine, code, own_second, other_second]
        specs = [whole, code_spec, matrix_spec(1), matrix_spec(1)]
        if out is not None:
            operands.append(out)
            specs.append(pl.BlockSpec(memory_space=pl.ANY))
        out = call(
            last_body, (1,), specs, row_spec(c), jax.ShapeDtypeStruct((columns, coeffs), jnp.float32),
            [matrix_scratch], cost(rows, 1, 10 * rows * coeffs + matrix_bytes),
            {} if out is None else {5: 0},
        )(*operands)
    return out


def solution(mesh):
    names = ("wide", "narrow_0", "narrow_1")
    torus = Mesh(mesh.devices.reshape(mesh.shape["wide"], 2, mesh.shape["narrow"] // 2), names)
    in_specs = (P(NARROW, "wide"), P(None, "wide", NARROW, None))
    out_specs = P(NARROW, "wide")
    return jax.shard_map(
        on_device, mesh=torus, in_specs=in_specs, out_specs=out_specs, check_vma=False
    )
```

```python
import functools

import jax
import jax.numpy as jnp
from jax import lax
from jax.experimental import pallas as pl
from jax.experimental.pallas import tpu as pltpu
from jax.sharding import Mesh
from jax.sharding import PartitionSpec as P

NARROW = ("narrow_0", "narrow_1")
FLOOR = 2.0 ** -3.875
SPAN = 2.0 ** 3.875 - 2.0 ** -3.875
LANES = 128
SCALE_ROWS = 16


def swapped(shard, axis, apart):
    return lax.ppermute(shard, axis, [(i, i ^ 1 << apart) for i in range(lax.axis_size(axis))])


def assemble(matrix, level, own_ref, other_refs, half, part):
    parts, _, blocks, rows, _ = own_ref.shape
    for block in range(blocks):
        for k in range(parts):
            start = pl.multiple_of((half * parts + k) * rows, rows)
            matrix[level, block, pl.ds(start, rows), :] = own_ref[k, level, block]
            place = (1 - half) * parts + ((part + (parts - k)) & (parts - 1))
            start = pl.multiple_of(place * rows, rows)
            matrix[level, block, pl.ds(start, rows), :] = other_refs[k][level, block]


def split(x):
    high = x.astype(jnp.bfloat16)
    return jnp.concatenate([high, (x - high.astype(jnp.float32)).astype(jnp.bfloat16)], axis=0)


def product(parts, matrix):
    dims = (((1,), (1,)), ((), ()))
    dots = lax.dot_general(parts, matrix, dims, preferred_element_type=jnp.float32)
    rows = parts.shape[0] // 2
    return dots[:rows] + dots[rows:]


def encode(value, out_ref):
    rows, columns = value.shape
    top = jnp.max(jnp.abs(value), axis=1, keepdims=True)
    top = jnp.maximum(jnp.broadcast_to(top, (rows, LANES)) * 1.01, 1e-30).astype(jnp.bfloat16)
    top = top.astype(jnp.float32)
    square = jnp.concatenate([top] * (LANES // rows), axis=0)
    out_ref[pl.ds(rows * (columns // LANES), SCALE_ROWS), :] = square.T[:SCALE_ROWS].astype(jnp.bfloat16)
    gain = SPAN / top
    for tile in range(columns // LANES):
        x = value[:, tile * LANES:(tile + 1) * LANES]
        t = jnp.abs(x) * gain + FLOOR
        for _ in range(5):
            t = t * t
        out_ref[pl.ds(tile * rows, rows), :] = jnp.where(x < 0, -t, t).astype(jnp.bfloat16)


def decode(code_ref, rows, columns):
    tiles = columns // LANES
    top = code_ref[pl.ds(rows * tiles, SCALE_ROWS), :].astype(jnp.float32)
    gain = jnp.broadcast_to(top[:1], (LANES, LANES)).T[:rows] * (1.0 / SPAN)
    values = []
    for tile in range(tiles):
        g = code_ref[pl.ds(tile * rows, rows), :].astype(jnp.float32)
        t = jnp.exp(jnp.log(jnp.abs(g)) * (1.0 / 32.0))
        y = (t - FLOOR) * gain
        values.append(jnp.where(g < 0, -y, y))
    return jnp.concatenate(values, axis=1)


def blocks_of(value, count, size):
    return [split(value[:, k * size:(k + 1) * size]) for k in range(count)]


def local_body(bits_ref, x_ref, own, *rest):
    others, out_ref, matrix = rest[:-2], rest[-2], rest[-1]
    levels, count, size = matrix.shape[:3]
    value = x_ref[...]
    for level in range(levels):
        assemble(matrix, level, own, others, bits_ref[0], bits_ref[1])
        parts = blocks_of(value, count, size)
        outs = []
        for k in range(count):
            low, high = parts[k & ~(1 << level)], parts[k | 1 << level]
            outs.append(
                product(low, matrix[level, k, :, :size]) + product(high, matrix[level, k, :, size:])
            )
        value = jnp.concatenate(outs, axis=1)
    out_ref[...] = value


def prepare_body(bits_ref, own, *rest):
    assemble(rest[-1], 0, own, rest[:-1], bits_ref[0], bits_ref[1])


def cross_level(mine, partner, matrix, upper):
    _, count, size, _ = matrix.shape
    own_parts, partner_parts = blocks_of(mine, count, size), blocks_of(partner, count, size)
    own_at = pl.multiple_of(upper * size, size)
    partner_at = pl.multiple_of((1 - upper) * size, size)
    outs = []
    for k in range(count):
        outs.append(
            product(own_parts[k], matrix[0, k, :, pl.ds(own_at, size)])
            + product(partner_parts[k], matrix[0, k, :, pl.ds(partner_at, size)])
        )
    return jnp.concatenate(outs, axis=1)


def core_body(bits_ref, mine_ref, partner_ref, matrix, out_ref, code_ref):
    value = cross_level(mine_ref[...], partner_ref[...], matrix, bits_ref[2])
    out_ref[...] = value
    encode(value, code_ref)


def middle_body(bits_ref, mine_ref, partner_ref, matrix, out_ref, code_ref):
    value = cross_level(mine_ref[...], decode(partner_ref, *mine_ref.shape), matrix, bits_ref[3])
    out_ref[...] = value
    encode(value, code_ref)


def last_body(bits_ref, mine_ref, partner_ref, matrix, *rest):
    rest[-1][...] = cross_level(mine_ref[...], decode(partner_ref, *mine_ref.shape), matrix, bits_ref[4])


def on_device(vectors, weights, chunks=8, window=2):
    columns, coeffs = vectors.shape
    _, count, share, width = weights.shape
    parts = lax.axis_size("narrow_1")
    rows = columns // chunks
    code_rows = rows * (coeffs // LANES) + SCALE_ROWS
    wide_top = lax.axis_size("wide").bit_length() - 1
    wide_bits = [0, wide_top // 2, wide_top - 1]
    place = lax.axis_index("wide")
    bits = jnp.stack(
        [lax.axis_index("narrow_0"), lax.axis_index("narrow_1")] + [place >> bit & 1 for bit in wide_bits]
    )

    def around(shard):
        return [shard] + [
            lax.ppermute(shard, "narrow_1", [(i, (i + k) % parts) for i in range(parts)]) for k in range(1, parts)
        ]

    own_early = lax.all_gather(weights[:3], "narrow_1")
    own_late = lax.all_gather(weights[3:], "narrow_1")
    first = swapped(weights[:2], "narrow_0", 0)
    turn, _ = lax.optimization_barrier((weights[2:4], first))
    second = swapped(turn, "narrow_0", 0)
    turn, _ = lax.optimization_barrier((weights[4:], second))
    third = swapped(turn, "narrow_0", 0)
    vectors, _ = lax.optimization_barrier((vectors, second))
    others = [around(first), around(second[:1]), around(second[1:]), around(third)]

    def call(body, in_specs, out_specs, out_shape, scratch, estimate, aliases={}):
        return pl.pallas_call(
            body,
            grid_spec=pltpu.PrefetchScalarGridSpec(
                num_scalar_prefetch=1, grid=(1,), in_specs=in_specs, out_specs=out_specs, scratch_shapes=scratch
            ),
            out_shape=out_shape,
            input_output_aliases=aliases,
            cost_estimate=estimate,
            compiler_params=pltpu.CompilerParams(vmem_limit_bytes=48 << 20),
        )

    def cost(rows_done, levels, bytes_accessed):
        return pl.CostEstimate(
            flops=4 * levels * rows_done * coeffs * width, bytes_accessed=bytes_accessed, transcendentals=0
        )

    size = width // 2
    matrix_bytes = 2 * count * size * width
    matrix_shape = (1, count, size, width)

    def gathered_spec(levels, at):
        return pl.BlockSpec((parts, levels, count, share, width), lambda i, bits: (0, at, 0, 0, 0))

    def shard_spec(levels, at):
        return pl.BlockSpec((levels, count, share, width), lambda i, bits: (at, 0, 0, 0))

    def prepared(own, own_at, other, other_at):
        return call(
            prepare_body, [gathered_spec(1, own_at)] + [shard_spec(1, other_at)] * parts,
            pl.BlockSpec(matrix_shape, lambda i, bits: (0, 0, 0, 0)),
            jax.ShapeDtypeStruct(matrix_shape, weights.dtype), [], cost(0, 0, 2 * matrix_bytes),
        )(bits, own, *other)

    def row_spec(index):
        return pl.BlockSpec((rows, coeffs), lambda i, bits: (index, 0))

    matrix_spec = pl.BlockSpec(matrix_shape, lambda i, bits: (0, 0, 0, 0))
    full = pl.BlockSpec((columns, coeffs), lambda i, bits: (0, 0))
    code_spec = pl.BlockSpec((code_rows, LANES), lambda i, bits: (0, 0))
    code_shape = jax.ShapeDtypeStruct((code_rows, LANES), jnp.bfloat16)
    chunk_shape = jax.ShapeDtypeStruct((rows, coeffs), jnp.float32)
    full_shape = jax.ShapeDtypeStruct((columns, coeffs), jnp.float32)

    current = call(
        local_body, [full, gathered_spec(2, 0)] + [shard_spec(2, 0)] * parts, full, full_shape,
        [pltpu.VMEM((2,) + matrix_shape[1:], weights.dtype)], cost(columns, 2, 8 * columns * coeffs + 2 * matrix_bytes),
    )(bits, vectors, own_early, *others[0])
    sent, _ = lax.optimization_barrier((current, others[1]))
    partner = swapped(sent, "wide", wide_bits[0])
    matrix = prepared(own_early, 2, others[1], 0)

    pieces = []
    for c in range(chunks):
        mine, code = call(
            core_body, [row_spec(c), row_spec(c), matrix_spec], [row_spec(0), code_spec],
            [chunk_shape, code_shape], [], cost(rows, 1, 14 * rows * coeffs + matrix_bytes),
        )(bits, current, partner, matrix)
        if c >= window:
            code, _ = lax.optimization_barrier((code, pieces[c - window][1]))
        pieces.append((mine, swapped(code, "wide", wide_bits[1])))
    matrix = prepared(own_late, 0, others[2], 0)
    later = []
    for mine, code in pieces:
        mine, code = call(
            middle_body, [row_spec(0), code_spec, matrix_spec], [row_spec(0), code_spec],
            [chunk_shape, code_shape], [], cost(rows, 1, 12 * rows * coeffs + matrix_bytes),
        )(bits, mine, code, matrix)
        later.append((mine, swapped(code, "wide", wide_bits[2])))
    matrix = prepared(own_late, 1, others[3], 0)
    out = None
    for c, (mine, code) in enumerate(later):
        operands = [bits, mine, code, matrix]
        specs = [row_spec(0), code_spec, matrix_spec]
        if out is not None:
            operands.append(out)
            specs.append(pl.BlockSpec(memory_space=pl.ANY))
        out = call(
            last_body, specs, row_spec(c), full_shape, [], cost(rows, 1, 10 * rows * coeffs + matrix_bytes),
            {} if out is None else {4: 0},
        )(*operands)
    return out


def solution(mesh):
    names = ("wide", "narrow_0", "narrow_1")
    torus = Mesh(mesh.devices.reshape(mesh.shape["wide"], 2, mesh.shape["narrow"] // 2), names)
    in_specs = (P(NARROW, "wide"), P(None, "wide", NARROW, None))
    out_specs = P(NARROW, "wide")
    return jax.shard_map(
        on_device, mesh=torus, in_specs=in_specs, out_specs=out_specs, check_vma=False
    )
```

```python
import functools

import jax
import jax.numpy as jnp
from jax import lax
from jax.experimental import pallas as pl
from jax.experimental.pallas import tpu as pltpu
from jax.sharding import Mesh
from jax.sharding import PartitionSpec as P

NARROW = ("narrow_0", "narrow_1")
FLOOR = 2.0 ** -3.875
SPAN = 2.0 ** 3.875 - 2.0 ** -3.875
LANES = 128
SCALE_ROWS = 16


def swapped(shard, axis, apart):
    return lax.ppermute(shard, axis, [(i, i ^ 1 << apart) for i in range(lax.axis_size(axis))])


def assembling(pairs, sems, half):
    copies = []
    for own_ref, other_ref, at, matrix_ref in pairs:
        parts, _, _, rows, _ = own_ref.shape
        for part in range(parts):
            for ref, side in ((own_ref, half), (other_ref, 1 - half)):
                start = pl.multiple_of((side * parts + part) * rows, rows)
                copies.append(
                    pltpu.make_async_copy(
                        ref.at[part, at], matrix_ref.at[:, pl.ds(start, rows), :], sems.at[len(copies)]
                    )
                )
    return copies


def split(x):
    high = x.astype(jnp.bfloat16)
    return jnp.concatenate([high, (x - high.astype(jnp.float32)).astype(jnp.bfloat16)], axis=0)


def product(parts, matrix):
    dims = (((1,), (1,)), ((), ()))
    dots = lax.dot_general(parts, matrix, dims, preferred_element_type=jnp.float32)
    rows = parts.shape[0] // 2
    return dots[:rows] + dots[rows:]


def encode(value, out_ref):
    rows, columns = value.shape
    top = jnp.max(jnp.abs(value), axis=1, keepdims=True)
    top = jnp.maximum(jnp.broadcast_to(top, (rows, LANES)) * 1.01, 1e-30).astype(jnp.bfloat16)
    top = top.astype(jnp.float32)
    square = jnp.concatenate([top] * (LANES // rows), axis=0)
    out_ref[pl.ds(rows * (columns // LANES), SCALE_ROWS), :] = square.T[:SCALE_ROWS].astype(jnp.bfloat16)
    gain = SPAN / top
    for tile in range(columns // LANES):
        x = value[:, tile * LANES:(tile + 1) * LANES]
        t = jnp.abs(x) * gain + FLOOR
        for _ in range(5):
            t = t * t
        out_ref[pl.ds(tile * rows, rows), :] = jnp.where(x < 0, -t, t).astype(jnp.bfloat16)


def decode(code_ref, rows, columns):
    tiles = columns // LANES
    top = code_ref[pl.ds(rows * tiles, SCALE_ROWS), :].astype(jnp.float32)
    gain = jnp.broadcast_to(top[:1], (LANES, LANES)).T[:rows] * (1.0 / SPAN)
    values = []
    for tile in range(tiles):
        g = code_ref[pl.ds(tile * rows, rows), :].astype(jnp.float32)
        t = jnp.exp(jnp.log(jnp.abs(g)) * (1.0 / 32.0))
        y = (t - FLOOR) * gain
        values.append(jnp.where(g < 0, -y, y))
    return jnp.concatenate(values, axis=1)


def blocks_of(value, count, size):
    return [split(value[:, k * size:(k + 1) * size]) for k in range(count)]


def local_body(bits_ref, x_ref, own, other, out_ref, next_ref, matrix, sems):
    levels, count, size = matrix.shape[:3]
    pairs = [(own, other, level, matrix.at[level]) for level in range(levels)] + [(own, other, levels, next_ref)]
    copies = assembling(pairs, sems, bits_ref[0])
    each = len(copies) // len(pairs)
    for copy in copies:
        copy.start()
    value = x_ref[...]
    for level in range(levels):
        for copy in copies[level * each:(level + 1) * each]:
            copy.wait()
        parts = blocks_of(value, count, size)
        outs = []
        for k in range(count):
            low, high = parts[k & ~(1 << level)], parts[k | 1 << level]
            outs.append(
                product(low, matrix[level, k, :, :size]) + product(high, matrix[level, k, :, size:])
            )
        value = jnp.concatenate(outs, axis=1)
    out_ref[...] = value
    for copy in copies[levels * each:]:
        copy.wait()


def prepare_body(bits_ref, own, other, *rest):
    outs, sems = rest[:-1], rest[-1]
    copies = assembling([(own, other, at, ref) for at, ref in enumerate(outs)], sems, bits_ref[0])
    for copy in copies:
        copy.start()
    for copy in copies:
        copy.wait()


def cross_level(mine, partner, matrix, upper):
    count, size, _ = matrix.shape
    own_parts, partner_parts = blocks_of(mine, count, size), blocks_of(partner, count, size)
    own_at = pl.multiple_of(upper * size, size)
    partner_at = pl.multiple_of((1 - upper) * size, size)
    outs = []
    for k in range(count):
        outs.append(
            product(own_parts[k], matrix[k, :, pl.ds(own_at, size)])
            + product(partner_parts[k], matrix[k, :, pl.ds(partner_at, size)])
        )
    return jnp.concatenate(outs, axis=1)


def core_body(bits_ref, mine_ref, partner_ref, matrix, out_ref, code_ref):
    value = cross_level(mine_ref[...], partner_ref[...], matrix, bits_ref[2])
    out_ref[...] = value
    encode(value, code_ref)


def middle_body(bits_ref, mine_ref, partner_ref, matrix, out_ref, code_ref):
    value = cross_level(mine_ref[...], decode(partner_ref, *mine_ref.shape), matrix, bits_ref[3])
    out_ref[...] = value
    encode(value, code_ref)


def last_body(bits_ref, mine_ref, partner_ref, matrix, *rest):
    rest[-1][...] = cross_level(mine_ref[...], decode(partner_ref, *mine_ref.shape), matrix, bits_ref[4])


def on_device(vectors, weights, chunks=4, window=2):
    columns, coeffs = vectors.shape
    _, count, share, width = weights.shape
    parts = lax.axis_size("narrow_1")
    rows = columns // chunks
    code_rows = rows * (coeffs // LANES) + SCALE_ROWS
    wide_top = lax.axis_size("wide").bit_length() - 1
    wide_bits = [0, wide_top // 2, wide_top - 1]
    place = lax.axis_index("wide")
    bits = jnp.stack(
        [lax.axis_index("narrow_0"), lax.axis_index("narrow_1")] + [place >> bit & 1 for bit in wide_bits]
    )

    def around(shard):
        return lax.all_to_all(jnp.broadcast_to(shard[None], (parts,) + shard.shape), "narrow_1", 0, 0)

    early, late = lax.optimization_barrier((weights[:3], weights[3:]))
    own_early = lax.all_gather(early, "narrow_1")
    own_late = lax.all_gather(late, "narrow_1")
    early_other = swapped(early, "narrow_0", 0)
    late_turn, _ = lax.optimization_barrier((late, early_other))
    late_other = swapped(late_turn, "narrow_0", 0)
    other_early = around(early_other)

    def call(body, in_specs, out_specs, out_shape, scratch, estimate, aliases={}):
        return pl.pallas_call(
            body,
            grid_spec=pltpu.PrefetchScalarGridSpec(
                num_scalar_prefetch=1, grid=(1,), in_specs=in_specs, out_specs=out_specs, scratch_shapes=scratch
            ),
            out_shape=out_shape,
            input_output_aliases=aliases,
            cost_estimate=estimate,
            compiler_params=pltpu.CompilerParams(vmem_limit_bytes=48 << 20),
        )

    def cost(rows_done, levels, bytes_accessed):
        return pl.CostEstimate(
            flops=4 * levels * rows_done * coeffs * width, bytes_accessed=bytes_accessed, transcendentals=0
        )

    size = width // 2
    matrix_bytes = 2 * count * size * width
    matrix_shape = (count, size, width)

    def row_spec(index):
        return pl.BlockSpec((rows, coeffs), lambda i, bits: (index, 0))

    matrix_spec = pl.BlockSpec(matrix_shape, lambda i, bits: (0, 0, 0))
    anywhere = pl.BlockSpec(memory_space=pl.ANY)
    matrix_type = jax.ShapeDtypeStruct(matrix_shape, weights.dtype)
    full = pl.BlockSpec((columns, coeffs), lambda i, bits: (0, 0))
    code_spec = pl.BlockSpec((code_rows, LANES), lambda i, bits: (0, 0))
    code_shape = jax.ShapeDtypeStruct((code_rows, LANES), jnp.bfloat16)
    chunk_shape = jax.ShapeDtypeStruct((rows, coeffs), jnp.float32)
    full_shape = jax.ShapeDtypeStruct((columns, coeffs), jnp.float32)

    current, matrix = call(
        local_body, [full, anywhere, anywhere], [full, anywhere], [full_shape, matrix_type],
        [pltpu.VMEM((2,) + matrix_shape, weights.dtype), pltpu.SemaphoreType.DMA((6 * parts,))],
        cost(columns, 2, 8 * columns * coeffs + 4 * matrix_bytes),
    )(bits, vectors, own_early, other_early)
    sent, late_other = lax.optimization_barrier((current, late_other))
    partner = swapped(sent, "wide", wide_bits[0])
    other_late = around(late_other)

    owns, codes = [], []
    for c in range(chunks):
        mine, code = call(
            core_body, [row_spec(c), row_spec(c), matrix_spec], [row_spec(0), code_spec],
            [chunk_shape, code_shape], [], cost(rows, 1, 14 * rows * coeffs + matrix_bytes),
        )(bits, current, partner, matrix)
        owns.append(mine)
        codes.append(code)
    arrived, later = [], []

    def middle(c):
        mine, code = call(
            middle_body, [row_spec(0), code_spec, matrix_spec], [row_spec(0), code_spec],
            [chunk_shape, code_shape], [], cost(rows, 1, 12 * rows * coeffs + matrix_bytes),
        )(bits, owns[c], arrived[c], middle_matrix)
        later.append((mine, code, swapped(code, "wide", wide_bits[2])))

    for c in range(chunks):
        code = codes[c]
        if c >= window:
            code, _ = lax.optimization_barrier((code, [arrived[c - window], codes[-1]]))
        arrived.append(swapped(code, "wide", wide_bits[1]))
    own_late, other_late, _ = lax.optimization_barrier((own_late, other_late, arrived[window - 1]))
    middle_matrix, last_matrix = call(
        prepare_body, [anywhere] * 2, [anywhere] * 2, [matrix_type] * 2, [pltpu.SemaphoreType.DMA((4 * parts,))],
        cost(0, 0, 4 * matrix_bytes),
    )(bits, own_late, other_late)
    for c in range(chunks):
        middle(c)
    later = [(mine, code) for mine, _, code in later]
    out = None
    for c, (mine, code) in enumerate(later):
        operands = [bits, mine, code, last_matrix]
        specs = [row_spec(0), code_spec, matrix_spec]
        if out is not None:
            operands.append(out)
            specs.append(pl.BlockSpec(memory_space=pl.ANY))
        out = call(
            last_body, specs, row_spec(c), full_shape, [], cost(rows, 1, 10 * rows * coeffs + matrix_bytes),
            {} if out is None else {4: 0},
        )(*operands)
    return out


def solution(mesh):
    names = ("wide", "narrow_0", "narrow_1")
    torus = Mesh(mesh.devices.reshape(mesh.shape["wide"], 2, mesh.shape["narrow"] // 2), names)
    in_specs = (P(NARROW, "wide"), P(None, "wide", NARROW, None))
    out_specs = P(NARROW, "wide")
    return jax.shard_map(
        on_device, mesh=torus, in_specs=in_specs, out_specs=out_specs, check_vma=False
    )
```

```python
import functools

import jax
import jax.numpy as jnp
from jax import lax
from jax.experimental import pallas as pl
from jax.experimental.pallas import tpu as pltpu
from jax.sharding import Mesh
from jax.sharding import PartitionSpec as P

NARROW = ("narrow_0", "narrow_1")
FLOOR = 2.0 ** -3.875
SPAN = 2.0 ** 3.875 - 2.0 ** -3.875
LANES = 128
SCALE_ROWS = 16


def swapped(shard, axis, apart):
    return lax.ppermute(shard, axis, [(i, i ^ 1 << apart) for i in range(lax.axis_size(axis))])


def assembling(pairs, sems, half):
    copies = []
    for own_ref, other_ref, at, matrix_ref in pairs:
        parts, _, _, rows, _ = own_ref.shape
        for part in range(parts):
            for ref, place, side in ((own_ref, at, half), (other_ref, at + (own_ref is other_ref), 1 - half)):
                start = pl.multiple_of((side * parts + part) * rows, rows)
                copies.append(
                    pltpu.make_async_copy(
                        ref.at[part, place], matrix_ref.at[:, pl.ds(start, rows), :], sems.at[len(copies)]
                    )
                )
    return copies


def split(x):
    high = x.astype(jnp.bfloat16)
    return jnp.concatenate([high, (x - high.astype(jnp.float32)).astype(jnp.bfloat16)], axis=0)


def product(parts, matrix):
    dims = (((1,), (1,)), ((), ()))
    dots = lax.dot_general(parts, matrix, dims, preferred_element_type=jnp.float32)
    rows = parts.shape[0] // 2
    return dots[:rows] + dots[rows:]


def encode(value, out_ref):
    rows, columns = value.shape
    top = jnp.max(jnp.abs(value), axis=1, keepdims=True)
    top = jnp.maximum(jnp.broadcast_to(top, (rows, LANES)) * 1.01, 1e-30).astype(jnp.bfloat16)
    top = top.astype(jnp.float32)
    square = jnp.concatenate([top] * (LANES // rows), axis=0)
    out_ref[pl.ds(rows * (columns // LANES), SCALE_ROWS), :] = square.T[:SCALE_ROWS].astype(jnp.bfloat16)
    gain = SPAN / top
    for tile in range(columns // LANES):
        x = value[:, tile * LANES:(tile + 1) * LANES]
        t = jnp.abs(x) * gain + FLOOR
        for _ in range(5):
            t = t * t
        out_ref[pl.ds(tile * rows, rows), :] = jnp.where(x < 0, -t, t).astype(jnp.bfloat16)


def decode(code_ref, rows, columns):
    tiles = columns // LANES
    top = code_ref[pl.ds(rows * tiles, SCALE_ROWS), :].astype(jnp.float32)
    gain = jnp.broadcast_to(top[:1], (LANES, LANES)).T[:rows] * (1.0 / SPAN)
    values = []
    for tile in range(tiles):
        g = code_ref[pl.ds(tile * rows, rows), :].astype(jnp.float32)
        t = jnp.exp(jnp.log(jnp.abs(g)) * (1.0 / 32.0))
        y = (t - FLOOR) * gain
        values.append(jnp.where(g < 0, -y, y))
    return jnp.concatenate(values, axis=1)


def blocks_of(value, count, size):
    return [split(value[:, k * size:(k + 1) * size]) for k in range(count)]


def local_body(bits_ref, x_ref, own, other, out_ref, next_ref, matrix, sems):
    levels, count, size = matrix.shape[:3]
    pairs = [(own, other, level, matrix.at[level]) for level in range(levels)] + [(own, other, levels, next_ref)]
    copies = assembling(pairs, sems, bits_ref[0])
    each = len(copies) // len(pairs)
    for copy in copies:
        copy.start()
    value = x_ref[...]
    for level in range(levels):
        for copy in copies[level * each:(level + 1) * each]:
            copy.wait()
        parts = blocks_of(value, count, size)
        outs = []
        for k in range(count):
            low, high = parts[k & ~(1 << level)], parts[k | 1 << level]
            outs.append(
                product(low, matrix[level, k, :, :size]) + product(high, matrix[level, k, :, size:])
            )
        value = jnp.concatenate(outs, axis=1)
    out_ref[...] = value
    for copy in copies[levels * each:]:
        copy.wait()


def prepare_body(bits_ref, gathered, *rest):
    outs, sems = rest[:-1], rest[-1]
    copies = assembling([(gathered, gathered, 2 * level, ref) for level, ref in enumerate(outs)], sems, bits_ref[0])
    for copy in copies:
        copy.start()
    for copy in copies:
        copy.wait()


def cross_level(mine, partner, matrix, upper):
    count, size, _ = matrix.shape
    own_parts, partner_parts = blocks_of(mine, count, size), blocks_of(partner, count, size)
    own_at = pl.multiple_of(upper * size, size)
    partner_at = pl.multiple_of((1 - upper) * size, size)
    outs = []
    for k in range(count):
        outs.append(
            product(own_parts[k], matrix[k, :, pl.ds(own_at, size)])
            + product(partner_parts[k], matrix[k, :, pl.ds(partner_at, size)])
        )
    return jnp.concatenate(outs, axis=1)


def core_body(bits_ref, mine_ref, partner_ref, matrix, out_ref, code_ref):
    value = cross_level(mine_ref[...], partner_ref[...], matrix, bits_ref[2])
    out_ref[...] = value
    encode(value, code_ref)


def middle_body(bits_ref, mine_ref, partner_ref, matrix, out_ref, code_ref):
    value = cross_level(mine_ref[...], decode(partner_ref, *mine_ref.shape), matrix, bits_ref[3])
    out_ref[...] = value
    encode(value, code_ref)


def last_body(bits_ref, mine_ref, partner_ref, matrix, *rest):
    rest[-1][...] = cross_level(mine_ref[...], decode(partner_ref, *mine_ref.shape), matrix, bits_ref[4])


def on_device(vectors, weights, chunks=4, window=2):
    columns, coeffs = vectors.shape
    _, count, share, width = weights.shape
    parts = lax.axis_size("narrow_1")
    rows = columns // chunks
    code_rows = rows * (coeffs // LANES) + SCALE_ROWS
    wide_top = lax.axis_size("wide").bit_length() - 1
    wide_bits = [0, wide_top // 2, wide_top - 1]
    place = lax.axis_index("wide")
    bits = jnp.stack(
        [lax.axis_index("narrow_0"), lax.axis_index("narrow_1")] + [place >> bit & 1 for bit in wide_bits]
    )

    def around(shard):
        return lax.all_to_all(jnp.broadcast_to(shard[None], (parts,) + shard.shape), "narrow_1", 0, 0)

    early, late = lax.optimization_barrier((weights[:3], weights[3:]))
    own_early = lax.all_gather(early, "narrow_1")
    early_other = swapped(early, "narrow_0", 0)
    late_turn, _ = lax.optimization_barrier((late, early_other))
    late_other = swapped(late_turn, "narrow_0", 0)
    other_early = around(early_other)

    def call(body, in_specs, out_specs, out_shape, scratch, estimate, aliases={}):
        return pl.pallas_call(
            body,
            grid_spec=pltpu.PrefetchScalarGridSpec(
                num_scalar_prefetch=1, grid=(1,), in_specs=in_specs, out_specs=out_specs, scratch_shapes=scratch
            ),
            out_shape=out_shape,
            input_output_aliases=aliases,
            cost_estimate=estimate,
            compiler_params=pltpu.CompilerParams(vmem_limit_bytes=48 << 20),
        )

    def cost(rows_done, levels, bytes_accessed):
        return pl.CostEstimate(
            flops=0, bytes_accessed=0, transcendentals=0
        )

    size = width // 2
    matrix_bytes = 2 * count * size * width
    matrix_shape = (count, size, width)

    def row_spec(index):
        return pl.BlockSpec((rows, coeffs), lambda i, bits: (index, 0))

    matrix_spec = pl.BlockSpec(matrix_shape, lambda i, bits: (0, 0, 0))
    anywhere = pl.BlockSpec(memory_space=pl.ANY)
    matrix_type = jax.ShapeDtypeStruct(matrix_shape, weights.dtype)
    full = pl.BlockSpec((columns, coeffs), lambda i, bits: (0, 0))
    code_spec = pl.BlockSpec((code_rows, LANES), lambda i, bits: (0, 0))
    code_shape = jax.ShapeDtypeStruct((code_rows, LANES), jnp.bfloat16)
    chunk_shape = jax.ShapeDtypeStruct((rows, coeffs), jnp.float32)
    full_shape = jax.ShapeDtypeStruct((columns, coeffs), jnp.float32)

    current, matrix = call(
        local_body, [full, anywhere, anywhere], [full, anywhere], [full_shape, matrix_type],
        [pltpu.VMEM((2,) + matrix_shape, weights.dtype), pltpu.SemaphoreType.DMA((6 * parts,))],
        cost(columns, 2, 8 * columns * coeffs + 4 * matrix_bytes),
    )(bits, vectors, own_early, other_early)
    sent, late_other = lax.optimization_barrier((current, late_other))
    partner = swapped(sent, "wide", wide_bits[0])

    owns, codes = [], []
    for c in range(chunks):
        mine, code = call(
            core_body, [row_spec(c), row_spec(c), matrix_spec], [row_spec(0), code_spec],
            [chunk_shape, code_shape], [], cost(rows, 1, 14 * rows * coeffs + matrix_bytes),
        )(bits, current, partner, matrix)
        owns.append(mine)
        codes.append(code)
    arrived, later = [], []

    def middle(c):
        mine, code = call(
            middle_body, [row_spec(0), code_spec, matrix_spec], [row_spec(0), code_spec],
            [chunk_shape, code_shape], [], cost(rows, 1, 12 * rows * coeffs + matrix_bytes),
        )(bits, owns[c], arrived[c], middle_matrix)
        later.append((mine, code, swapped(code, "wide", wide_bits[2])))

    late_other, _ = lax.optimization_barrier((late_other, codes[1]))
    gathered = lax.all_gather(jnp.stack([late, late_other], 1).reshape(-1, *late.shape[1:]), "narrow_1")
    middle_matrix, last_matrix = call(
        prepare_body, [anywhere], [anywhere] * 2, [matrix_type] * 2, [pltpu.SemaphoreType.DMA((4 * parts,))],
        cost(0, 0, 4 * matrix_bytes),
    )(bits, gathered)
    for c in range(chunks):
        code = codes[c]
        if c >= window:
            code, _ = lax.optimization_barrier((code, gathered))
        arrived.append(swapped(code, "wide", wide_bits[1]))
    for c in range(chunks):
        middle(c)
    later = [(mine, code) for mine, _, code in later]
    out = None
    for c, (mine, code) in enumerate(later):
        operands = [bits, mine, code, last_matrix]
        specs = [row_spec(0), code_spec, matrix_spec]
        if out is not None:
            operands.append(out)
            specs.append(pl.BlockSpec(memory_space=pl.ANY))
        out = call(
            last_body, specs, row_spec(c), full_shape, [], cost(rows, 1, 10 * rows * coeffs + matrix_bytes),
            {} if out is None else {4: 0},
        )(*operands)
    return out


def solution(mesh):
    names = ("wide", "narrow_0", "narrow_1")
    torus = Mesh(mesh.devices.reshape(mesh.shape["wide"], 2, mesh.shape["narrow"] // 2), names)
    in_specs = (P(NARROW, "wide"), P(None, "wide", NARROW, None))
    out_specs = P(NARROW, "wide")
    return jax.shard_map(
        on_device, mesh=torus, in_specs=in_specs, out_specs=out_specs, check_vma=False
    )
```

```python
import functools

import jax
import jax.numpy as jnp
from jax import lax
from jax.experimental import pallas as pl
from jax.experimental.pallas import tpu as pltpu
from jax.sharding import Mesh
from jax.sharding import PartitionSpec as P

NARROW = ("narrow_0", "narrow_1")
FLOOR = 2.0 ** -3.875
SPAN = 2.0 ** 3.875 - 2.0 ** -3.875
LANES = 128
SCALE_ROWS = 16


def swapped(shard, axis, apart):
    return lax.ppermute(shard, axis, [(i, i ^ 1 << apart) for i in range(lax.axis_size(axis))])


def assembling(pairs, sems, half):
    copies = []
    for own_ref, other_ref, at, matrix_ref in pairs:
        parts, _, _, rows, _ = own_ref.shape
        for part in range(parts):
            for ref, place, side in ((own_ref, at, half), (other_ref, at + (own_ref is other_ref), 1 - half)):
                start = pl.multiple_of((side * parts + part) * rows, rows)
                copies.append(
                    pltpu.make_async_copy(
                        ref.at[part, place], matrix_ref.at[:, pl.ds(start, rows), :], sems.at[len(copies)]
                    )
                )
    return copies


def split(x):
    high = x.astype(jnp.bfloat16)
    return jnp.concatenate([high, (x - high.astype(jnp.float32)).astype(jnp.bfloat16)], axis=0)


def product(parts, matrix):
    dims = (((1,), (1,)), ((), ()))
    dots = lax.dot_general(parts, matrix, dims, preferred_element_type=jnp.float32)
    rows = parts.shape[0] // 2
    return dots[:rows] + dots[rows:]


def encode(value, out_ref):
    rows, columns = value.shape
    top = jnp.max(jnp.abs(value), axis=1, keepdims=True)
    top = jnp.maximum(jnp.broadcast_to(top, (rows, LANES)) * 1.01, 1e-30).astype(jnp.bfloat16)
    top = top.astype(jnp.float32)
    square = jnp.concatenate([top] * (LANES // rows), axis=0)
    out_ref[pl.ds(rows * (columns // LANES), SCALE_ROWS), :] = square.T[:SCALE_ROWS].astype(jnp.bfloat16)
    gain = SPAN / top
    for tile in range(columns // LANES):
        x = value[:, tile * LANES:(tile + 1) * LANES]
        t = jnp.abs(x) * gain + FLOOR
        for _ in range(5):
            t = t * t
        out_ref[pl.ds(tile * rows, rows), :] = jnp.where(x < 0, -t, t).astype(jnp.bfloat16)


def decode(code_ref, rows, columns):
    tiles = columns // LANES
    top = code_ref[pl.ds(rows * tiles, SCALE_ROWS), :].astype(jnp.float32)
    gain = jnp.broadcast_to(top[:1], (LANES, LANES)).T[:rows] * (1.0 / SPAN)
    values = []
    for tile in range(tiles):
        g = code_ref[pl.ds(tile * rows, rows), :].astype(jnp.float32)
        t = jnp.exp(jnp.log(jnp.abs(g)) * (1.0 / 32.0))
        y = (t - FLOOR) * gain
        values.append(jnp.where(g < 0, -y, y))
    return jnp.concatenate(values, axis=1)


def blocks_of(value, count, size):
    return [split(value[:, k * size:(k + 1) * size]) for k in range(count)]


def local_body(bits_ref, x_ref, own, other, out_ref, next_ref, matrix, sems):
    levels, count, size = matrix.shape[:3]
    parts, _, _, rows, _ = own.shape
    copies = assembling([(own, other, levels, next_ref)], sems, bits_ref[0])
    for copy in copies:
        copy.start()
    value = x_ref[...]
    for level in range(levels):
        for part in range(parts):
            for ref, side in ((own, bits_ref[0]), (other, 1 - bits_ref[0])):
                start = pl.multiple_of((side * parts + part) * rows, rows)
                matrix[level, :, pl.ds(start, rows), :] = ref[part, level]
        pieces = blocks_of(value, count, size)
        outs = []
        for k in range(count):
            low, high = pieces[k & ~(1 << level)], pieces[k | 1 << level]
            outs.append(
                product(low, matrix[level, k, :, :size]) + product(high, matrix[level, k, :, size:])
            )
        value = jnp.concatenate(outs, axis=1)
    out_ref[...] = value
    for copy in copies:
        copy.wait()


def prepare_body(bits_ref, gathered, *rest):
    outs, sems = rest[:-1], rest[-1]
    copies = assembling([(gathered, gathered, 2 * level, ref) for level, ref in enumerate(outs)], sems, bits_ref[0])
    for copy in copies:
        copy.start()
    for copy in copies:
        copy.wait()


def cross_level(mine, partner, matrix, upper):
    count, size, _ = matrix.shape
    own_parts, partner_parts = blocks_of(mine, count, size), blocks_of(partner, count, size)
    own_at = pl.multiple_of(upper * size, size)
    partner_at = pl.multiple_of((1 - upper) * size, size)
    outs = []
    for k in range(count):
        outs.append(
            product(own_parts[k], matrix[k, :, pl.ds(own_at, size)])
            + product(partner_parts[k], matrix[k, :, pl.ds(partner_at, size)])
        )
    return jnp.concatenate(outs, axis=1)


def core_body(bits_ref, mine_ref, partner_ref, matrix, out_ref, code_ref):
    value = cross_level(mine_ref[...], partner_ref[...], matrix, bits_ref[2])
    out_ref[...] = value
    encode(value, code_ref)


def middle_body(bits_ref, mine_ref, partner_ref, matrix, out_ref, code_ref):
    value = cross_level(mine_ref[...], decode(partner_ref, *mine_ref.shape), matrix, bits_ref[3])
    out_ref[...] = value
    encode(value, code_ref)


def last_body(bits_ref, mine_ref, partner_ref, matrix, *rest):
    rest[-1][...] = cross_level(mine_ref[...], decode(partner_ref, *mine_ref.shape), matrix, bits_ref[4])


def on_device(vectors, weights, chunks=4, window=2):
    columns, coeffs = vectors.shape
    _, count, share, width = weights.shape
    parts = lax.axis_size("narrow_1")
    rows = columns // chunks
    code_rows = rows * (coeffs // LANES) + SCALE_ROWS
    wide_top = lax.axis_size("wide").bit_length() - 1
    wide_bits = [0, wide_top // 2, wide_top - 1]
    place = lax.axis_index("wide")
    bits = jnp.stack(
        [lax.axis_index("narrow_0"), lax.axis_index("narrow_1")] + [place >> bit & 1 for bit in wide_bits]
    )

    def around(shard):
        return lax.all_to_all(jnp.broadcast_to(shard[None], (parts,) + shard.shape), "narrow_1", 0, 0)

    early, late = weights[:3], weights[3:]
    own_early = lax.all_gather(early, "narrow_1")
    early_other = swapped(early, "narrow_0", 0)
    late_turn, _ = lax.optimization_barrier((late, early_other))
    late_other = swapped(late_turn, "narrow_0", 0)
    other_early = around(early_other)

    def call(body, in_specs, out_specs, out_shape, scratch, estimate, aliases={}):
        return pl.pallas_call(
            body,
            grid_spec=pltpu.PrefetchScalarGridSpec(
                num_scalar_prefetch=1, grid=(1,), in_specs=in_specs, out_specs=out_specs, scratch_shapes=scratch
            ),
            out_shape=out_shape,
            input_output_aliases=aliases,
            cost_estimate=estimate,
            compiler_params=pltpu.CompilerParams(vmem_limit_bytes=48 << 20),
        )

    def cost(rows_done, levels, bytes_accessed):
        return pl.CostEstimate(
            flops=0, bytes_accessed=0, transcendentals=0
        )

    size = width // 2
    matrix_bytes = 2 * count * size * width
    matrix_shape = (count, size, width)

    def in_hbm(array):
        return pltpu.with_memory_space_constraint(array, pltpu.HBM)

    def row_spec(index):
        return pl.BlockSpec((rows, coeffs), lambda i, bits: (index, 0))

    matrix_spec = pl.BlockSpec(matrix_shape, lambda i, bits: (0, 0, 0))
    anywhere = pl.BlockSpec(memory_space=pl.ANY)
    in_vmem = pl.BlockSpec(memory_space=pltpu.VMEM)
    matrix_type = jax.ShapeDtypeStruct(matrix_shape, weights.dtype)
    full = pl.BlockSpec((columns, coeffs), lambda i, bits: (0, 0))
    code_spec = pl.BlockSpec((code_rows, LANES), lambda i, bits: (0, 0))
    code_shape = jax.ShapeDtypeStruct((code_rows, LANES), jnp.bfloat16)
    chunk_shape = jax.ShapeDtypeStruct((rows, coeffs), jnp.float32)
    full_shape = jax.ShapeDtypeStruct((columns, coeffs), jnp.float32)

    current, matrix = call(
        local_body, [full, in_vmem, in_vmem], [full, anywhere], [full_shape, matrix_type],
        [pltpu.VMEM((2,) + matrix_shape, weights.dtype), pltpu.SemaphoreType.DMA((2 * parts,))],
        cost(columns, 2, 8 * columns * coeffs + 4 * matrix_bytes),
    )(bits, vectors, own_early, other_early)
    sent, late_other = lax.optimization_barrier((current, late_other))
    partner = swapped(sent, "wide", wide_bits[0])

    owns, codes = [], []
    for c in range(chunks):
        mine, code = call(
            core_body, [row_spec(c), row_spec(c), matrix_spec], [row_spec(0), code_spec],
            [chunk_shape, code_shape], [], cost(rows, 1, 14 * rows * coeffs + matrix_bytes),
        )(bits, in_hbm(current), in_hbm(partner), matrix)
        owns.append(mine)
        codes.append(code)
    arrived, later = [], []

    def middle(c):
        mine, code = call(
            middle_body, [row_spec(0), code_spec, matrix_spec], [row_spec(0), code_spec],
            [chunk_shape, code_shape], [], cost(rows, 1, 12 * rows * coeffs + matrix_bytes),
        )(bits, owns[c], arrived[c], middle_matrix)
        later.append((mine, code, swapped(code, "wide", wide_bits[2])))

    late_other, _ = lax.optimization_barrier((late_other, codes[1]))
    gathered = lax.all_gather(jnp.stack([late, late_other], 1).reshape(-1, *late.shape[1:]), "narrow_1")
    middle_matrix, last_matrix = call(
        prepare_body, [anywhere], [anywhere] * 2, [matrix_type] * 2, [pltpu.SemaphoreType.DMA((4 * parts,))],
        cost(0, 0, 4 * matrix_bytes),
    )(bits, gathered)
    for c in range(chunks):
        code = codes[c]
        if c >= window:
            code, _ = lax.optimization_barrier((code, gathered))
        arrived.append(swapped(code, "wide", wide_bits[1]))
    for c in range(chunks):
        middle(c)
    later = [(mine, code) for mine, _, code in later]
    out = None
    for c, (mine, code) in enumerate(later):
        operands = [bits, mine, code, last_matrix]
        specs = [row_spec(0), code_spec, matrix_spec]
        if out is not None:
            operands.append(out)
            specs.append(pl.BlockSpec(memory_space=pl.ANY))
        out = call(
            last_body, specs, row_spec(c), full_shape, [], cost(rows, 1, 10 * rows * coeffs + matrix_bytes),
            {} if out is None else {4: 0},
        )(*operands)
    return out


def solution(mesh):
    names = ("wide", "narrow_0", "narrow_1")
    torus = Mesh(mesh.devices.reshape(mesh.shape["wide"], 2, mesh.shape["narrow"] // 2), names)
    in_specs = (P(NARROW, "wide"), P(None, "wide", NARROW, None))
    out_specs = P(NARROW, "wide")
    return jax.shard_map(
        on_device, mesh=torus, in_specs=in_specs, out_specs=out_specs, check_vma=False
    )
```
